512 devices in a mesh: strip: 128 (over z, x, core), frames: 4 (over y).
Axes of the slice: x: 4, y: 4, z: 16, core: 2. Of those that a mesh axis runs over, the one named last changes fastest.
Arguments:
- frames: float32 [512, 512, 512], P('frames', 'strip'), may hold values from -6 to 6
- kernel: float32 [2, 512, 512], P(None, 'frames', 'strip'), may hold values from -6 to 6
- owner_rank: int32 [4, 128], P('frames'), may hold values from 0 to 127, each once within a row
- block_ids: int32 [512, 16], P('frames'), may hold values from 0 to 63
- block_counts: int32 [512], P('frames'), may hold values from 1 to 16, 4096 in all
Outputs:
- disk_blocks: float32 [128, 64, 4096], P('strip', 'frames')
The draws below stay inside these ranges and needn't reach their ends.
Inputs may be any that keep to these rules, and one draw needn't show every extreme that they name: `owner_rank`: each row lists every rank of a group once; owner s of a group owns the one frame of rank s. `block_ids`: slots at or beyond a frame's count are unused. `block_counts`: some frame uses all 16 slots.
All inputs are finite; a program needn't handle non-finite values. No bound on the sum of `block_counts` on one device may be relied on, other than what follows from the above.
Results may differ from the reference program's by a relative error of at most 0.0003.
Values sent between devices are 32-bit elements; how exact they have to be, the bound alone decides.
A program may use at most 64 MiB of HBM per device.

```python
import math
import jax
import jax.numpy as jnp
import numpy as np
from jax import lax

DET = 512
BLK = 64
NB = 8
MAXB = 16
FPO = 1
FR_LOC = 128
FRAMES = 512
N_STRIP = 128
N_FRAMES = 4


def plant(entries, own_key, smallest, top_value):
    longest = entries.shape.index(max(entries.shape))
    spots = []
    for shift in (0, 1):
        where = [jax.random.randint(jax.random.fold_in(own_key, axis), (), 0, length) for axis, length in enumerate(entries.shape)]
        where[longest] = (where[longest] + shift) % entries.shape[longest]
        spots.append(tuple(where))
    return entries.at[spots[0]].set(smallest).at[spots[1]].set(top_value)


def shard_levels(rng, dims, pieces, low, largest):
    def one(dim, parts):
        steps = jax.random.uniform(jax.random.fold_in(jax.random.fold_in(rng, 6), dim), (parts,), jnp.float32, low / len(pieces), largest / len(pieces))
        return jnp.repeat(jnp.exp(steps), dims[dim] // parts).reshape((-1,) + (1,) * (len(dims) - dim - 1))

    factor_of = one(*pieces[0])
    for cut in pieces[1:]:
        factor_of = factor_of * one(*cut)
    return factor_of


def split_up(amount, total, reach, slope):
    portions = [(1 << 20) // math.isqrt(standing ** slope) + 1 for standing in range(2, amount + 1)]
    spare, counts = total - reach - (amount - 1), [1] * (amount - 1)
    while spare > 0:
        candidates = [i for i in range(amount - 1) if counts[i] < reach]
        pool, left = sum([portions[i] for i in candidates]), spare
        for i in candidates:
            addition = min(reach - counts[i], max(1, left * portions[i] // pool), spare)
            counts[i] = counts[i] + addition
            spare = spare - addition
    return np.array([reach] + counts)


def ragged(key, number_of, total, most, skew):
    if number_of == 2:
        one = jax.random.randint(key, (), max(1, total - most), min(most, total - 1) + 1)
        return jnp.stack([one, total - one])
    sizes = jnp.asarray(split_up(number_of, total, most, skew), jnp.int32)
    couples = (number_of - 1) // 2
    source_of, receiver = sizes[1:1 + 2 * couples:2], sizes[2:2 + 2 * couples:2]
    room = jnp.minimum(source_of - 1, most - receiver)
    shifted = jax.random.randint(jax.random.fold_in(key, 1), (couples,), 0, 1 << 20) % (room + 1)
    sizes = sizes.at[1:1 + 2 * couples:2].set(source_of - shifted).at[2:2 + 2 * couples:2].set(receiver + shifted)
    return sizes[jax.random.permutation(jax.random.fold_in(key, 2), number_of)]


def scatter_about(stream_key, dims, spread, most, pieces=(), kind=jnp.bfloat16):
    drawn = spread * jax.random.normal(stream_key, dims, jnp.float32)
    if pieces:
        drawn = drawn * shard_levels(stream_key, dims, pieces, -0.22, 0.18)
    return jnp.clip(drawn, -most, most).astype(kind)


def setup_inputs(seed: int = 0) -> dict:
    splits = jax.random.split(jax.random.key(seed), 6)
    frames = scatter_about(splits[0], (FRAMES, DET, DET), 1.0, 6.0, ((0, 4), (1, 128)), jnp.float32)
    kernel = scatter_about(splits[1], (2, DET, DET), 1.0, 6.0, ((1, 4), (2, 128)), jnp.float32)
    owner_rank = jax.vmap(lambda own: jax.random.permutation(own, FR_LOC))(jax.random.split(splits[2], N_FRAMES)).reshape((N_FRAMES, FR_LOC)).astype(jnp.int32)
    block_ids = plant(jax.random.randint(splits[3], (FRAMES, MAXB), 0, NB * NB), jax.random.fold_in(splits[3], 1), 0, (NB * NB) - 1).astype(jnp.int32)
    block_counts = ragged(splits[4], FRAMES, FRAMES * MAXB // 2, MAXB, 0).astype(jnp.int32)
    return {"frames": frames, "kernel": kernel, "owner_rank": owner_rank, "block_ids": block_ids, "block_counts": block_counts}


def corr_frame(frame, kernel_c):
    spectrum = jnp.fft.fft2(frame) * kernel_c
    return jnp.real(jnp.fft.ifft2(spectrum))


def reference(frames, kernel, owner_rank, block_ids, block_counts):
    kernel_c = kernel[0] + 1j * kernel[1]

    def frame_blocks(items):
        frame, frame_ids, frame_count = items
        correlation = corr_frame(frame, kernel_c)
        tile_rows = correlation.reshape(NB, BLK, NB, BLK).transpose(0, 2, 1, 3).reshape(NB * NB, BLK * BLK)
        picked = tile_rows[frame_ids]
        keep_mask = jnp.arange(MAXB, dtype=jnp.int32) < frame_count
        return jnp.where(keep_mask[:, None], picked, jnp.zeros_like(picked))

    per_frame = lax.map(frame_blocks, (frames, block_ids, block_counts))
    rank_list = owner_rank.reshape(-1)
    group_index = jnp.arange(N_FRAMES * FR_LOC, dtype=jnp.int32) // FR_LOC
    destination = (rank_list // FPO) * (N_FRAMES * FPO) + group_index * FPO + rank_list % FPO
    collected = jnp.zeros((N_STRIP * N_FRAMES * FPO, MAXB, BLK * BLK), per_frame.dtype).at[destination].set(per_frame)
    return collected.reshape(N_STRIP, N_FRAMES * FPO * MAXB, BLK * BLK)
```

```python
import functools

import jax
import jax.numpy as jnp
import ml_dtypes
import numpy as np
from jax import lax
from jax.experimental import pallas as pl
from jax.experimental.pallas import tpu as pltpu
from jax.sharding import Mesh
from jax.sharding import PartitionSpec as P

DET = 512
HALF = DET // 2
NB = 8
MAXB = 16
Z, X, C, Y = 16, 4, 2, 4
PLANE = X * C
STRIPS = Z * PLANE
STRIP = ("z", "x", "c")
U = 272
AHEAD = 2
F32 = jnp.float32
BF16 = jnp.bfloat16
MESH = pl.DeviceIdType.MESH


def offset_of(k):
    h = Z // 2 - (k + 1) // 2
    return (h * (1 - 2 * (k % 2))) % Z


def halves(table):
    high = table.astype(ml_dtypes.bfloat16)
    low = (table - high.astype(np.float64)).astype(ml_dtypes.bfloat16)
    return high, low


def tables():
    n = np.arange(DET)
    angle = 2.0 * np.pi / DET
    u = np.arange(U)
    used = (u <= HALF).astype(np.float64)[:, None]
    rows = np.concatenate([(-offset_of(k) % Z) * 32 + np.arange(32) for k in range(Z)])
    phase = (u[:, None] * rows[None, :]) % DET * angle
    forward = np.concatenate([np.cos(phase) * used, -np.sin(phase) * used])
    forward = forward.reshape(2 * U, 2, HALF).transpose(1, 0, 2)
    j = np.arange(HALF)
    small = (j[:, None] * j[None, :]) % HALF * (2.0 * angle)
    square = np.concatenate([np.cos(small), np.sin(small)], axis=1)
    turn = np.zeros((8, DET))
    turn[0] = np.concatenate([np.cos(j * angle), np.sin(j * angle)])
    out_rows = np.concatenate([n[0::2], n[1::2]])
    weight = np.where(j == 0, 1.0, 2.0) / (DET * DET)
    back = (out_rows[:, None] * j[None, :]) % DET * angle
    inverse = np.concatenate([np.cos(back) * weight, -np.sin(back) * weight], axis=1)
    jj, cc, xx, zz = np.meshgrid(np.arange(4), np.arange(C), np.arange(X), np.arange(Z), indexing="ij")
    v_in = (4 * (8 * zz + 2 * xx + cc) + jj).reshape(-1)
    v_out = np.concatenate([n[0::2], n[1::2]])
    pick = np.concatenate(
        [(n[None, :] == u[:, None]) * used, (n[None, :] == (-u[:, None]) % DET) * used]
    )
    place = np.concatenate(
        [v_in[:, None] == v_out[None, :], v_in[:, None] == (-v_out[None, :]) % DET]
    )
    wide = np.concatenate([*halves(forward[0]), *halves(forward[1])])
    return (
        wide,
        np.concatenate([*halves(square), *halves(inverse), (0.5 * place).astype(ml_dtypes.bfloat16),
                        pick.astype(ml_dtypes.bfloat16)]),
        turn.astype(np.float32),
    )


def remote(src, dst, send_sem, recv_sem, **where):
    return pltpu.make_async_remote_copy(
        src_ref=src, dst_ref=dst, send_sem=send_sem, recv_sem=recv_sem, device_id=where, device_id_type=MESH
    )


def wait_bytes(view, sem):
    pltpu.make_async_copy(view, view, sem).wait()


def split(value):
    high = value.astype(BF16)
    return high, (value - high.astype(F32)).astype(BF16)


def mul(left, right):
    return jnp.dot(left, right, preferred_element_type=F32)


def body(owner_frame, frames_hbm, kernel_hbm, wide_hbm, square_hbm, turn_hbm, plane,
         frames, staged, mid, rows, kern, wide, square, turn, spec, folded,
         in_sem, tab_sem, send_p, recv_p, send_z, recv_z, send_k, recv_kz, recv_kx, recv_ky, recv_kc):
    z, x, c, y = (lax.axis_index(a) for a in ("z", "x", "c", "y"))
    mine = x * C + c
    load = pltpu.make_async_copy(frames_hbm, frames, in_sem.at[0])
    load.start()
    own_rows = pl.ds(pl.multiple_of(y * 1024 + ((c * X + x) * Z + z) * 8, 8), 8)
    load_kernel = pltpu.make_async_copy(kernel_hbm, kern.at[own_rows], in_sem.at[1])
    load_kernel.start()

    peers = [{"x": (x + p // C) % X, "c": (c + p % C) % C} for p in range(1, PLANE)]
    peers += [{"z": (z + d) % Z} for d in range(1, Z)]
    peers += [{"y": (y + d) % Y} for d in range(1, Y)]
    barrier = pltpu.get_barrier_semaphore()
    for peer in peers:
        pl.semaphore_signal(barrier, inc=1, device_id=peer, device_id_type=MESH)
    pl.semaphore_wait(barrier, len(peers))

    load_kernel.wait()
    for d in range(1, Z):
        remote(kern.at[own_rows], kern.at[own_rows], send_k, recv_kz, z=(z + d) % Z).start()
    load.wait()

    def to_plane(k):
        base = ((z + offset_of(k)) % Z) * PLANE
        for p in range(1, PLANE):
            xx, cc = (x + p // C) % X, (c + p % C) % C
            slot = k * PLANE + p
            staged[slot] = frames[owner_frame[base + xx * C + cc]]
            remote(staged.at[slot], mid.at[k * PLANE + mine], send_p, recv_p.at[k], x=xx, c=cc).start()
        mid[k * PLANE + mine] = frames[owner_frame[base + mine]]

    def from_plane(k):
        wait_bytes(mid.at[pl.ds(k * PLANE, PLANE - 1)], recv_p.at[k])

    def along_z(k):
        piece = pl.ds(k * PLANE, PLANE)
        remote(mid.at[piece], rows.at[piece], send_z, recv_z.at[k // 8], z=(z + offset_of(k)) % Z).start()

    def step(k, carry):
        to_plane(k + AHEAD)
        from_plane(k)
        along_z(k)
        return carry

    for k in range(AHEAD):
        to_plane(k)
    lax.fori_loop(0, 3, step, 0)
    third = pl.ds(pl.multiple_of(y * 1024 + (c * X + x) * 128, 128), 128)
    wait_bytes(kern.at[pl.ds(0, 120)], recv_kz)
    for d in range(1, X):
        remote(kern.at[third], kern.at[third], send_k, recv_kx, x=(x + d) % X).start()
    lax.fori_loop(3, 7, step, 0)
    second = pl.ds(pl.multiple_of(y * 1024 + c * 512, 512), 512)
    wait_bytes(kern.at[pl.ds(0, 384)], recv_kx)
    for d in range(1, Y):
        remote(kern.at[second], kern.at[second], send_k, recv_ky.at[d], y=(y + d) % Y).start()
    remote(kern.at[second], kern.at[second], send_k, recv_kc.at[0], c=1 - c).start()
    lax.fori_loop(7, Z - AHEAD, step, 0)
    from_plane(Z - 2)
    along_z(Z - 2)
    from_plane(Z - 1)
    last = pl.ds((Z - 1) * PLANE, PLANE)
    rows[last] = mid[last]

    loads = [
        pltpu.make_async_copy(wide_hbm, wide, tab_sem.at[0]),
        pltpu.make_async_copy(square_hbm, square, tab_sem.at[1]),
        pltpu.make_async_copy(turn_hbm, turn, tab_sem.at[2]),
    ]
    for table in loads:
        table.start()
    for d in range(1, Y):
        view = kern.at[pl.ds(pl.multiple_of((y + Y - d) % Y * 1024 + c * 512, 512), 512)]
        wait_bytes(view, recv_ky.at[d])
        remote(view, view, send_k, recv_kc.at[d], c=1 - c).start()
    for table in loads:
        table.wait()
    for d in range(Y):
        wait_bytes(kern.at[pl.ds(0, 512)], recv_kc.at[d])

    first = []
    for part in range(2):
        t = jnp.concatenate(
            [
                jnp.concatenate(
                    [kern[pl.ds(yy * 1024 + part * 4 + jj, 128, stride=8), :] for jj in range(4)], axis=0
                )
                for yy in range(Y)
            ],
            axis=1,
        )
        high, low = split(t)
        dims = (((1,), (1,)), ((), ()))
        pick = square[pl.ds(2560, 2 * U), :]
        picked = lax.dot_general(pick, high, dims, preferred_element_type=F32)
        picked = picked + lax.dot_general(pick, low, dims, preferred_element_type=F32)
        first.append(picked)
    for sign in range(2):
        stack = jnp.concatenate([f[sign * U:(sign + 1) * U] for f in first], axis=0)
        high, low = split(stack)
        place = square[pl.ds(1536 + sign * DET, DET), :]
        moved = mul(high, place) + mul(low, place)
        if sign == 0:
            folded[...] = moved
        else:
            folded[pl.ds(0, U), :] += moved[:U]
            folded[pl.ds(U, U), :] -= moved[U:]

    def over_rows(g):
        high, low = split(rows[pl.ds(g * 64, 64)].reshape(HALF, DET))
        w_high = wide[pl.ds(g * 4 * U, 2 * U), :]
        w_low = wide[pl.ds(g * 4 * U + 2 * U, 2 * U), :]
        return mul(w_high, high) + mul(w_high, low) + mul(w_low, high)

    wait_bytes(rows.at[pl.ds(0, 64)], recv_z.at[0])
    spec[...] = over_rows(0)
    wait_bytes(rows.at[pl.ds(0, 56)], recv_z.at[1])
    total = spec[...] + over_rows(1)

    t_high, t_low = square[pl.ds(0, HALF), :], square[pl.ds(HALF, HALF), :]
    tc, ts = turn[0:1, :HALF], turn[0:1, HALF:]

    def square_product(parts):
        high, low = split(jnp.concatenate(parts, axis=0))
        full = mul(high, t_high) + mul(low, t_high) + mul(high, t_low)
        return [(full[i * U:(i + 1) * U, :HALF], full[i * U:(i + 1) * U, HALF:]) for i in range(4)]

    re, im = total[:U], total[U:]
    a_re, a_im = re[:, :HALF] + re[:, HALF:], im[:, :HALF] + im[:, HALF:]
    b_re, b_im = re[:, :HALF] - re[:, HALF:], im[:, :HALF] - im[:, HALF:]
    q = square_product([a_re, a_im, b_re * tc + b_im * ts, b_im * tc - b_re * ts])
    products = []
    for side in range(2):
        f_re = q[2 * side][0] + q[2 * side + 1][1]
        f_im = q[2 * side + 1][0] - q[2 * side][1]
        cols = pl.ds(side * HALF, HALF)
        k_re, k_im = folded[pl.ds(0, U), cols], folded[pl.ds(U, U), cols]
        products += [f_re * k_re - f_im * k_im, f_re * k_im + f_im * k_re]
    q = square_product(products)
    a_re, a_im = q[0][0] - q[1][1], q[1][0] + q[0][1]
    o_re, o_im = q[2][0] - q[3][1], q[3][0] + q[2][1]
    b_re, b_im = o_re * tc - o_im * ts, o_im * tc + o_re * ts
    middle = (a_re[HALF:HALF + 1], b_re[HALF:HALF + 1])
    nyquist = jnp.concatenate([middle[0] + middle[1], middle[0] - middle[1]], axis=1) * (1.0 / (DET * DET))
    a_re, a_im, b_re, b_im = (v[:HALF] for v in (a_re, a_im, b_re, b_im))
    stack = jnp.concatenate(
        [
            jnp.concatenate([a_re + b_re, a_re - b_re], axis=1),
            jnp.concatenate([a_im + b_im, a_im - b_im], axis=1),
        ],
        axis=0,
    )
    high, low = split(stack)
    i_high, i_low = square[pl.ds(512, DET), :], square[pl.ds(1024, DET), :]
    result = mul(i_high, high) + mul(i_high, low) + mul(i_low, high)
    even, odd = result[:HALF] + nyquist, result[HALF:] - nyquist
    for t in range(4):
        plane[t, pl.ds(0, HALF), :] = even[:, t * 128:(t + 1) * 128]
        plane[t, pl.ds(HALF, HALF), :] = odd[:, t * 128:(t + 1) * 128]

    wait_bytes(staged.at[pl.ds(0, 112)], send_p)
    wait_bytes(mid.at[pl.ds(0, 120)], send_z)
    wait_bytes(kern.at[pl.ds(0, 120)], send_k)
    wait_bytes(kern.at[pl.ds(0, 384)], send_k)
    wait_bytes(kern.at[pl.ds(0, 3584)], send_k)


def select(owner_frame, ids, counts, plane, out, slots):
    z, x, c = (lax.axis_index(a) for a in STRIP)
    own = owner_frame[(z * X + x) * C + c]
    count = counts[own]
    left = lax.broadcasted_iota(jnp.int32, (16, 128), 1) < 64
    for m in range(MAXB):
        b = jnp.where(m < count, ids[m, own], 0)
        rb, cb = lax.div(b, NB), lax.rem(b, NB)
        lane_tile, lane_half = lax.div(cb, 2), lax.rem(cb, 2)
        for part in range(2):
            start = pl.multiple_of(lax.rem(rb * 32 + (Z - z) * 16 + part * 16, HALF), 16)
            e = plane[lane_tile, pl.ds(start, 16), :]
            o = plane[lane_tile, pl.ds(start + HALF, 16), :]
            low_pair = jnp.where(left, e, pltpu.roll(o, 64, 1))
            high_pair = jnp.where(left, pltpu.roll(e, 64, 1), o)
            pair = jnp.where(lane_half == 0, low_pair, high_pair)
            slots[pl.ds(m * 32 + part * 16, 16), :] = jnp.where(m < count, pair, 0.0)
    for r in range(32):
        out[:, pl.ds(r * 128, 128)] = slots[pl.ds(r, MAXB, stride=32), :]


def shards(frames, kernel, owner_rank, block_ids, block_counts):
    rank = owner_rank.reshape(-1)
    place = jnp.arange(STRIPS, dtype=jnp.int32)
    owner_frame = jnp.sum(jnp.where(rank[None, :] == place[:, None], place[None, :], 0), axis=1)
    wide, square, turn = tables()
    hbm = pl.BlockSpec(memory_space=pltpu.HBM)
    smem = pl.BlockSpec(memory_space=pltpu.SMEM)
    vmem = pl.BlockSpec(memory_space=pltpu.VMEM)
    dma = pltpu.SemaphoreType.DMA
    strips = (STRIPS, 4, DET)
    def in_hbm(array):
        return pltpu.with_memory_space_constraint(array, pltpu.HBM)

    plane = pl.pallas_call(
        body,
        name="correlate",
        out_shape=pltpu.VMEM((4, DET, 128), F32),
        in_specs=[smem, hbm, hbm, hbm, hbm, hbm],
        out_specs=vmem,
        scratch_shapes=[
            pltpu.VMEM(strips, F32),
            pltpu.VMEM(strips, F32),
            pltpu.VMEM(strips, F32),
            pltpu.VMEM(strips, F32),
            pltpu.VMEM((4096, 128), F32),
            pltpu.VMEM(wide.shape, BF16),
            pltpu.VMEM(square.shape, BF16),
            pltpu.VMEM(turn.shape, F32),
            pltpu.VMEM((2 * U, DET), F32),
            pltpu.VMEM((2 * U, DET), F32),
            dma((2,)), dma((3,)), dma, dma((Z,)), dma, dma((2,)), dma, dma, dma, dma((Y,)), dma((Y,)),
        ],
        compiler_params=pltpu.CompilerParams(
            collective_id=0, has_side_effects=True, vmem_limit_bytes=50 << 20
        ),
    )(
        owner_frame,
        in_hbm(frames),
        in_hbm(kernel.transpose(0, 2, 1).reshape(8, 128)),
        in_hbm(jnp.asarray(wide)),
        in_hbm(jnp.asarray(square)),
        in_hbm(jnp.asarray(turn)),
    )
    result = pl.pallas_call(
        select,
        name="select",
        out_shape=jax.ShapeDtypeStruct((MAXB, 4096), F32),
        in_specs=[smem, smem, smem, vmem],
        out_specs=vmem,
        scratch_shapes=[pltpu.VMEM((MAXB * 32, 128), F32)],
        compiler_params=pltpu.CompilerParams(vmem_limit_bytes=4 << 20),
    )(owner_frame, block_ids.T, block_counts, plane)
    return result[None]


def solution(mesh):
    finer = Mesh(mesh.devices.reshape(Z, X, C, Y), ("z", "x", "c", "y"))
    in_specs = (
        P("y", STRIP, None),
        P(None, "y", STRIP),
        P("y", None),
        P("y", None),
        P("y"),
    )
    return jax.shard_map(
        shards, mesh=finer, in_specs=in_specs, out_specs=P(STRIP, "y", None), check_vma=False
    )
```

```python
import functools

import jax
import jax.numpy as jnp
import ml_dtypes
import numpy as np
from jax import lax
from jax.experimental import pallas as pl
from jax.experimental.pallas import tpu as pltpu
from jax.sharding import Mesh
from jax.sharding import PartitionSpec as P

DET = 512
HALF = DET // 2
NB = 8
MAXB = 16
Z, X, C, Y = 16, 4, 2, 4
PLANE = X * C
STRIPS = Z * PLANE
STRIP = ("z", "x", "c")
U = 272
AHEAD = 2
FAR = 2
F32 = jnp.float32
BF16 = jnp.bfloat16
MESH = pl.DeviceIdType.MESH


def offset_of(k):
    h = Z // 2 - (k + 1) // 2
    return (h * (1 - 2 * (k % 2))) % Z


def halves(table):
    high = table.astype(ml_dtypes.bfloat16)
    low = (table - high.astype(np.float64)).astype(ml_dtypes.bfloat16)
    return high, low


def tables():
    n = np.arange(DET)
    angle = 2.0 * np.pi / DET
    u = np.arange(U)
    used = (u <= HALF).astype(np.float64)[:, None]
    rows = np.concatenate([(-offset_of(k) % Z) * 32 + np.arange(32) for k in range(Z)])
    phase = (u[:, None] * rows[None, :]) % DET * angle
    forward = np.concatenate([np.cos(phase) * used, -np.sin(phase) * used])
    forward = forward.reshape(2 * U, 2, HALF).transpose(1, 0, 2)
    j = np.arange(HALF)
    small = (j[:, None] * j[None, :]) % HALF * (2.0 * angle)
    square = np.block([[np.cos(small), -np.sin(small)], [np.sin(small), np.cos(small)]])
    turn = np.zeros((8, DET))
    turn[0] = np.concatenate([np.cos(j * angle), np.sin(j * angle)])
    out_rows = np.concatenate([n[0::2], n[1::2]])
    weight = np.where(j == 0, 1.0, 2.0) / (DET * DET)
    back = (out_rows[:, None] * j[None, :]) % DET * angle
    inverse = np.concatenate([np.cos(back) * weight, -np.sin(back) * weight], axis=1)
    jj, cc, xx, zz = np.meshgrid(np.arange(4), np.arange(C), np.arange(X), np.arange(Z), indexing="ij")
    v_in = (4 * (8 * zz + 2 * xx + cc) + jj).reshape(-1)
    v_out = np.concatenate([n[0::2], n[1::2]])
    pick = np.concatenate(
        [(n[None, :] == u[:, None]) * used, (n[None, :] == (-u[:, None]) % DET) * used]
    )
    place = np.concatenate(
        [v_in[:, None] == v_out[None, :], v_in[:, None] == (-v_out[None, :]) % DET]
    )
    wide = np.concatenate([*halves(forward[0]), *halves(forward[1])])
    return (
        wide,
        np.concatenate([*halves(square), *halves(inverse), (0.5 * place).astype(ml_dtypes.bfloat16),
                        pick.astype(ml_dtypes.bfloat16)]),
        turn.astype(np.float32),
    )


def remote(src, dst, send_sem, recv_sem, **where):
    return pltpu.make_async_remote_copy(
        src_ref=src, dst_ref=dst, send_sem=send_sem, recv_sem=recv_sem, device_id=where, device_id_type=MESH
    )


def wait_bytes(view, sem):
    pltpu.make_async_copy(view, view, sem).wait()


def split(value):
    high = value.astype(BF16)
    return high, (value - high.astype(F32)).astype(BF16)


def mul(left, right):
    return jnp.dot(left, right, preferred_element_type=F32)


def body(owner_frame, frames_hbm, kernel_hbm, wide_hbm, square_hbm, turn_hbm, plane,
         frames, staged, mid, far, rows, kern, wide, square, turn, spec, folded,
         in_sem, tab_sem, send_p, recv_p, send_z, recv_z, recv_far, recv_out, send_k, recv_kz, recv_kx, recv_ky, recv_kc):
    z, x, c, y = (lax.axis_index(a) for a in ("z", "x", "c", "y"))
    mine = x * C + c
    load = pltpu.make_async_copy(frames_hbm, frames, in_sem.at[0])
    load.start()
    own_rows = pl.ds(pl.multiple_of(y * 1024 + ((c * X + x) * Z + z) * 8, 8), 8)
    load_kernel = pltpu.make_async_copy(kernel_hbm, kern.at[own_rows], in_sem.at[1])
    load_kernel.start()

    peers = [{"z": (z + offset_of(k)) % Z} for k in range(Z - 1)]
    peers += [{"x": (x + p // C) % X, "c": (c + p % C) % C} for p in range(1, PLANE)]
    peers += [{"y": (y + d) % Y} for d in range(1, Y)]
    barrier = pltpu.get_barrier_semaphore()
    for peer in peers:
        pl.semaphore_signal(barrier, inc=1, device_id=peer, device_id_type=MESH)
    pl.semaphore_wait(barrier, len(peers))

    load_kernel.wait()
    for d in range(1, Z):
        remote(kern.at[own_rows], kern.at[own_rows], send_k, recv_kz, z=(z + d) % Z).start()
    load.wait()

    def far_first(k):
        there = (z + offset_of(k)) % Z
        for p in range(PLANE):
            staged[k * PLANE + p] = frames[owner_frame[there * PLANE + p]]
        remote(staged.at[pl.ds(k * PLANE, PLANE)], far.at[k], send_z, recv_far.at[k], z=there).start()

    def to_plane(k):
        base = ((z + offset_of(k)) % Z) * PLANE
        for p in range(1, PLANE):
            xx, cc = (x + p // C) % X, (c + p % C) % C
            slot = k * PLANE + p
            staged[slot] = frames[owner_frame[base + xx * C + cc]]
            remote(staged.at[slot], mid.at[k * PLANE + mine], send_p, recv_p.at[k], x=xx, c=cc).start()
        mid[k * PLANE + mine] = frames[owner_frame[base + mine]]

    def from_plane(k):
        wait_bytes(mid.at[pl.ds(k * PLANE, PLANE - 1)], recv_p.at[k])

    def along_z(k):
        piece = pl.ds(k * PLANE, PLANE)
        remote(mid.at[piece], rows.at[piece], send_z, recv_z.at[k // 8], z=(z + offset_of(k)) % Z).start()

    def step(k, carry):
        to_plane(k + AHEAD)
        from_plane(k)
        along_z(k)
        return carry

    for k in range(FAR):
        far_first(k)
    for k in range(FAR, FAR + AHEAD):
        to_plane(k)
    lax.fori_loop(FAR, 5, step, 0)
    third = pl.ds(pl.multiple_of(y * 1024 + (c * X + x) * 128, 128), 128)
    wait_bytes(kern.at[pl.ds(0, 120)], recv_kz)
    for d in range(1, X):
        remote(kern.at[third], kern.at[third], send_k, recv_kx, x=(x + d) % X).start()
    lax.fori_loop(5, 8, step, 0)
    second = pl.ds(pl.multiple_of(y * 1024 + c * 512, 512), 512)
    wait_bytes(kern.at[pl.ds(0, 384)], recv_kx)
    for d in range(1, Y):
        remote(kern.at[second], kern.at[second], send_k, recv_ky.at[d], y=(y + d) % Y).start()
    remote(kern.at[second], kern.at[second], send_k, recv_kc.at[0], c=1 - c).start()
    lax.fori_loop(8, Z - AHEAD, step, 0)
    from_plane(Z - 2)
    along_z(Z - 2)
    from_plane(Z - 1)
    last = pl.ds((Z - 1) * PLANE, PLANE)
    rows[last] = mid[last]

    loads = [
        pltpu.make_async_copy(wide_hbm, wide, tab_sem.at[0]),
        pltpu.make_async_copy(square_hbm, square, tab_sem.at[1]),
        pltpu.make_async_copy(turn_hbm, turn, tab_sem.at[2]),
    ]
    for table in loads:
        table.start()
    for d in range(1, Y):
        view = kern.at[pl.ds(pl.multiple_of((y + Y - d) % Y * 1024 + c * 512, 512), 512)]
        wait_bytes(view, recv_ky.at[d])
        remote(view, view, send_k, recv_kc.at[d], c=1 - c).start()
    for k in range(FAR):
        wait_bytes(far.at[k], recv_far.at[k])
        for p in range(1, PLANE):
            xx, cc = (x + p // C) % X, (c + p % C) % C
            remote(far.at[k, xx * C + cc], rows.at[k * PLANE + mine], send_p, recv_out, x=xx, c=cc).start()
        rows[k * PLANE + mine] = far[k, mine]
    for table in loads:
        table.wait()
    for d in range(Y):
        wait_bytes(kern.at[pl.ds(0, 512)], recv_kc.at[d])

    first = []
    for part in range(2):
        t = jnp.concatenate(
            [
                jnp.concatenate(
                    [kern[pl.ds(yy * 1024 + part * 4 + jj, 128, stride=8), :] for jj in range(4)], axis=0
                )
                for yy in range(Y)
            ],
            axis=1,
        )
        high, low = split(t)
        dims = (((1,), (1,)), ((), ()))
        pick = square[pl.ds(3072, 2 * U), :]
        picked = lax.dot_general(pick, high, dims, preferred_element_type=F32)
        picked = picked + lax.dot_general(pick, low, dims, preferred_element_type=F32)
        first.append(picked)
    for sign in range(2):
        stack = jnp.concatenate([f[sign * U:(sign + 1) * U] for f in first], axis=0)
        high, low = split(stack)
        place = square[pl.ds(2048 + sign * DET, DET), :]
        moved = mul(high, place) + mul(low, place)
        if sign == 0:
            folded[...] = moved
        else:
            folded[pl.ds(0, U), :] += moved[:U]
            folded[pl.ds(U, U), :] -= moved[U:]

    def over_rows(g):
        high, low = split(rows[pl.ds(g * 64, 64)].reshape(HALF, DET))
        w_high = wide[pl.ds(g * 4 * U, 2 * U), :]
        w_low = wide[pl.ds(g * 4 * U + 2 * U, 2 * U), :]
        return mul(w_high, high) + mul(w_high, low) + mul(w_low, high)

    wait_bytes(rows.at[pl.ds(0, FAR * (PLANE - 1))], recv_out)
    wait_bytes(rows.at[pl.ds(0, 64 - FAR * PLANE)], recv_z.at[0])
    spec[...] = over_rows(0)
    wait_bytes(rows.at[pl.ds(0, 56)], recv_z.at[1])
    total = spec[...] + over_rows(1)

    t_high, t_low = square[pl.ds(0, DET), :], square[pl.ds(DET, DET), :]
    tc, ts = turn[0:1, :HALF], turn[0:1, HALF:]

    def two(first, second):
        high, low = split(jnp.concatenate([jnp.concatenate(first, axis=1), jnp.concatenate(second, axis=1)], axis=0))
        full = mul(high, t_high) + mul(low, t_high) + mul(high, t_low)
        return full[:U, :HALF], full[:U, HALF:], full[U:, :HALF], full[U:, HALF:]

    re, im = total[:U], total[U:]
    a_re, a_im = re[:, :HALF] + re[:, HALF:], im[:, :HALF] + im[:, HALF:]
    b_re, b_im = re[:, :HALF] - re[:, HALF:], im[:, :HALF] - im[:, HALF:]
    a_re, a_im, o_re, o_im = two([a_re, a_im], [b_re * tc + b_im * ts, b_im * tc - b_re * ts])
    k_re, k_im = folded[pl.ds(0, U), pl.ds(0, HALF)], folded[pl.ds(U, U), pl.ds(0, HALF)]
    l_re, l_im = folded[pl.ds(0, U), pl.ds(HALF, HALF)], folded[pl.ds(U, U), pl.ds(HALF, HALF)]
    a_im, a_re, o_im, o_re = two(
        [a_re * k_im + a_im * k_re, a_re * k_re - a_im * k_im],
        [o_re * l_im + o_im * l_re, o_re * l_re - o_im * l_im],
    )
    b_re, b_im = o_re * tc - o_im * ts, o_im * tc + o_re * ts
    middle = (a_re[HALF:HALF + 1], b_re[HALF:HALF + 1])
    nyquist = jnp.concatenate([middle[0] + middle[1], middle[0] - middle[1]], axis=1) * (1.0 / (DET * DET))
    a_re, a_im, b_re, b_im = (v[:HALF] for v in (a_re, a_im, b_re, b_im))
    stack = jnp.concatenate(
        [
            jnp.concatenate([a_re + b_re, a_re - b_re], axis=1),
            jnp.concatenate([a_im + b_im, a_im - b_im], axis=1),
        ],
        axis=0,
    )
    high, low = split(stack)
    i_high, i_low = square[pl.ds(1024, DET), :], square[pl.ds(1536, DET), :]
    result = mul(i_high, high) + mul(i_high, low) + mul(i_low, high)
    even, odd = result[:HALF] + nyquist, result[HALF:] - nyquist
    for t in range(4):
        plane[t, pl.ds(0, HALF), :] = even[:, t * 128:(t + 1) * 128]
        plane[t, pl.ds(HALF, HALF), :] = odd[:, t * 128:(t + 1) * 128]

    wait_bytes(staged.at[pl.ds(0, 112)], send_p)
    wait_bytes(mid.at[pl.ds(0, 120)], send_z)
    wait_bytes(kern.at[pl.ds(0, 120)], send_k)
    wait_bytes(kern.at[pl.ds(0, 384)], send_k)
    wait_bytes(kern.at[pl.ds(0, 3584)], send_k)


def select(owner_frame, ids, counts, plane, out, slots):
    z, x, c = (lax.axis_index(a) for a in STRIP)
    own = owner_frame[(z * X + x) * C + c]
    count = counts[own]
    left = lax.broadcasted_iota(jnp.int32, (16, 128), 1) < 64
    for m in range(MAXB):
        b = jnp.where(m < count, ids[m, own], 0)
        rb, cb = lax.div(b, NB), lax.rem(b, NB)
        lane_tile, lane_half = lax.div(cb, 2), lax.rem(cb, 2)
        for part in range(2):
            start = pl.multiple_of(lax.rem(rb * 32 + (Z - z) * 16 + part * 16, HALF), 16)
            e = plane[lane_tile, pl.ds(start, 16), :]
            o = plane[lane_tile, pl.ds(start + HALF, 16), :]
            low_pair = jnp.where(left, e, pltpu.roll(o, 64, 1))
            high_pair = jnp.where(left, pltpu.roll(e, 64, 1), o)
            pair = jnp.where(lane_half == 0, low_pair, high_pair)
            slots[pl.ds(m * 32 + part * 16, 16), :] = jnp.where(m < count, pair, 0.0)
    for r in range(32):
        out[:, pl.ds(r * 128, 128)] = slots[pl.ds(r, MAXB, stride=32), :]


def shards(frames, kernel, owner_rank, block_ids, block_counts):
    rank = owner_rank.reshape(-1)
    place = jnp.arange(STRIPS, dtype=jnp.int32)
    owner_frame = jnp.sum(jnp.where(rank[None, :] == place[:, None], place[None, :], 0), axis=1)
    wide, square, turn = tables()
    hbm = pl.BlockSpec(memory_space=pltpu.HBM)
    smem = pl.BlockSpec(memory_space=pltpu.SMEM)
    vmem = pl.BlockSpec(memory_space=pltpu.VMEM)
    dma = pltpu.SemaphoreType.DMA
    strips = (STRIPS, 4, DET)
    def in_hbm(array):
        return pltpu.with_memory_space_constraint(array, pltpu.HBM)

    plane = pl.pallas_call(
        body,
        name="correlate",
        out_shape=pltpu.VMEM((4, DET, 128), F32),
        in_specs=[smem, hbm, hbm, hbm, hbm, hbm],
        out_specs=vmem,
        scratch_shapes=[
            pltpu.VMEM(strips, F32),
            pltpu.VMEM(strips, F32),
            pltpu.VMEM(strips, F32),
            pltpu.VMEM((FAR, PLANE, 4, DET), F32),
            pltpu.VMEM(strips, F32),
            pltpu.VMEM((4096, 128), F32),
            pltpu.VMEM(wide.shape, BF16),
            pltpu.VMEM(square.shape, BF16),
            pltpu.VMEM(turn.shape, F32),
            pltpu.VMEM((2 * U, DET), F32),
            pltpu.VMEM((2 * U, DET), F32),
            dma((2,)), dma((3,)), dma, dma((Z,)), dma, dma((2,)), dma((FAR,)), dma, dma, dma, dma, dma((Y,)), dma((Y,)),
        ],
        compiler_params=pltpu.CompilerParams(
            collective_id=0, has_side_effects=True, vmem_limit_bytes=50 << 20
        ),
    )(
        owner_frame,
        in_hbm(frames),
        in_hbm(kernel.transpose(0, 2, 1).reshape(8, 128)),
        in_hbm(jnp.asarray(wide)),
        in_hbm(jnp.asarray(square)),
        in_hbm(jnp.asarray(turn)),
    )
    result = pl.pallas_call(
        select,
        name="select",
        out_shape=jax.ShapeDtypeStruct((MAXB, 4096), F32),
        in_specs=[smem, smem, smem, vmem],
        out_specs=vmem,
        scratch_shapes=[pltpu.VMEM((MAXB * 32, 128), F32)],
        compiler_params=pltpu.CompilerParams(vmem_limit_bytes=4 << 20),
    )(owner_frame, block_ids.T, block_counts, plane)
    return result[None]


def solution(mesh):
    finer = Mesh(mesh.devices.reshape(Z, X, C, Y), ("z", "x", "c", "y"))
    in_specs = (
        P("y", STRIP, None),
        P(None, "y", STRIP),
        P("y", None),
        P("y", None),
        P("y"),
    )
    return jax.shard_map(
        shards, mesh=finer, in_specs=in_specs, out_specs=P(STRIP, "y", None), check_vma=False
    )
```

```python
import functools

import jax
import jax.numpy as jnp
import ml_dtypes
import numpy as np
from jax import lax
from jax.experimental import pallas as pl
from jax.experimental.pallas import tpu as pltpu
from jax.sharding import Mesh
from jax.sharding import PartitionSpec as P

DET = 512
HALF = DET // 2
NB = 8
MAXB = 16
Z, X, C, Y = 16, 4, 2, 4
PLANE = X * C
STRIPS = Z * PLANE
STRIP = ("z", "x", "c")
U = 272
AHEAD = 9
FAR = (8, 9, 7, 10)
F32 = jnp.float32
BF16 = jnp.bfloat16
MESH = pl.DeviceIdType.MESH


def halves(table):
    high = table.astype(ml_dtypes.bfloat16)
    low = (table - high.astype(np.float64)).astype(ml_dtypes.bfloat16)
    return high, low


def tables():
    n = np.arange(DET)
    angle = 2.0 * np.pi / DET
    u = np.arange(U)
    used = (u <= HALF).astype(np.float64)[:, None]
    phase = (u[:, None] * n[None, :]) % DET * angle
    forward = np.concatenate([np.cos(phase) * used, -np.sin(phase) * used])
    forward = forward.reshape(2 * U, 2, HALF).transpose(1, 0, 2)
    j = np.arange(HALF)
    small = (j[:, None] * j[None, :]) % HALF * (2.0 * angle)
    square = np.block([[np.cos(small), -np.sin(small)], [np.sin(small), np.cos(small)]])
    turn = np.zeros((8, DET))
    turn[0] = np.concatenate([np.cos(j * angle), np.sin(j * angle)])
    out_rows = np.concatenate([n[0::2], n[1::2]])
    weight = np.where(j == 0, 1.0, 2.0) / (DET * DET)
    back = (out_rows[:, None] * j[None, :]) % DET * angle
    inverse = np.concatenate([np.cos(back) * weight, -np.sin(back) * weight], axis=1)
    jj, cc, xx, zz = np.meshgrid(np.arange(4), np.arange(C), np.arange(X), np.arange(Z), indexing="ij")
    v_in = (4 * (8 * zz + 2 * xx + cc) + jj).reshape(-1)
    v_out = np.concatenate([n[0::2], n[1::2]])
    pick = np.concatenate(
        [(n[None, :] == u[:, None]) * used, (n[None, :] == (-u[:, None]) % DET) * used]
    )
    place = np.concatenate(
        [v_in[:, None] == v_out[None, :], v_in[:, None] == (-v_out[None, :]) % DET]
    )
    wide = np.concatenate([*halves(forward[0]), *halves(forward[1])])
    return (
        wide,
        np.concatenate([*halves(square), *halves(inverse), (0.5 * place).astype(ml_dtypes.bfloat16),
                        pick.astype(ml_dtypes.bfloat16)]),
        turn.astype(np.float32),
    )


def remote(src, dst, send_sem, recv_sem, **where):
    return pltpu.make_async_remote_copy(
        src_ref=src, dst_ref=dst, send_sem=send_sem, recv_sem=recv_sem, device_id=where, device_id_type=MESH
    )


def wait_bytes(view, sem):
    pltpu.make_async_copy(view, view, sem).wait()


def split(value):
    high = value.astype(BF16)
    return high, (value - high.astype(F32)).astype(BF16)


def mul(left, right):
    return jnp.dot(left, right, preferred_element_type=F32)


def body(owner_frame, frames_hbm, kernel_hbm, wide_hbm, square_hbm, turn_hbm, plane,
         frames, staged, mid, far, rows, kern, wide, square, turn, spec, folded,
         in_sem, tab_sem, send_p, recv_p, send_z, recv_z, recv_far, recv_out, send_k, recv_kz, recv_kx, recv_ky, recv_kc):
    z, x, c, y = (lax.axis_index(a) for a in ("z", "x", "c", "y"))
    mine = x * C + c
    z_at = [z] + [lax.rem(z + d, Z) for d in range(1, Z)]
    y_at = [y] + [lax.rem(y + d, Y) for d in range(1, Y)]
    x_at = [x] + [lax.rem(x + d, X) for d in range(1, X)]
    plane_at = [(x_at[p // C], (c, 1 - c)[p % C]) for p in range(PLANE)]
    load = pltpu.make_async_copy(frames_hbm, frames, in_sem.at[0])
    load.start()
    own_rows = pl.ds(pl.multiple_of(y * 1024 + ((c * X + x) * Z + z) * 8, 8), 8)
    load_kernel = pltpu.make_async_copy(kernel_hbm, kern.at[own_rows], in_sem.at[1])
    load_kernel.start()

    peers = [{"z": z_at[d]} for d in range(1, Z)]
    peers += [{"x": xx, "c": cc} for xx, cc in plane_at[1:]]
    peers += [{"y": y_at[d]} for d in range(1, Y)]
    barrier = pltpu.get_barrier_semaphore()
    for peer in peers:
        pl.semaphore_signal(barrier, inc=1, device_id=peer, device_id_type=MESH)
    pl.semaphore_wait(barrier, len(peers))

    load_kernel.wait()
    for d in range(1, Z):
        remote(kern.at[own_rows], kern.at[own_rows], send_k, recv_kz, z=z_at[d]).start()
    load.wait()

    def far_first(k):
        there = z_at[FAR[k]]
        for p in range(PLANE):
            staged[there * PLANE + p] = frames[owner_frame[there * PLANE + p]]
        remote(staged.at[pl.ds(there * PLANE, PLANE)], far.at[k], send_z, recv_far.at[k], z=there).start()

    def is_near(t):
        away = (t - z + Z) % Z
        near = away != FAR[0]
        for d in FAR[1:]:
            near = jnp.logical_and(near, away != d)
        return near

    def target_of(k):
        i = k % 8
        return (z + Z + (i + 1) // 2 * (1 - 2 * (i % 2))) % (Z // 2) + Z // 2 * (k // (Z // 2))

    def to_plane(k):
        t = target_of(k)

        @pl.when(is_near(t))
        def _():
            for p in range(1, PLANE):
                xx, cc = plane_at[p]
                slot = t * PLANE + xx * C + cc
                staged[slot] = frames[owner_frame[slot]]
                remote(staged.at[slot], mid.at[t * PLANE + mine], send_p, recv_p.at[t], x=xx, c=cc).start()
            mid[t * PLANE + mine] = frames[owner_frame[t * PLANE + mine]]

    def onward(k):
        t = target_of(k)

        @pl.when(is_near(t))
        def _():
            piece = pl.ds(t * PLANE, PLANE)
            wait_bytes(mid.at[pl.ds(t * PLANE, PLANE - 1)], recv_p.at[t])
            slot = (z - t + Z) % Z

            @pl.when(t != z)
            def _():
                target = rows.at[pl.ds(slot * PLANE, PLANE)]
                remote(mid.at[piece], target, send_z, recv_z.at[slot // 8], z=t).start()

            @pl.when(t == z)
            def _():
                rows[pl.ds(0, PLANE)] = mid[piece]

    def step(t, carry):
        to_plane(t + AHEAD)
        onward(t)
        return carry

    for k in range(len(FAR)):
        far_first(k)
    for t in range(AHEAD):
        to_plane(t)
    lax.fori_loop(0, 2, step, 0)
    third = pl.ds(pl.multiple_of(y * 1024 + (c * X + x) * 128, 128), 128)
    wait_bytes(kern.at[pl.ds(0, 120)], recv_kz)
    for d in range(1, X):
        remote(kern.at[third], kern.at[third], send_k, recv_kx, x=x_at[d]).start()
    lax.fori_loop(2, 4, step, 0)
    second = pl.ds(pl.multiple_of(y * 1024 + c * 512, 512), 512)
    wait_bytes(kern.at[pl.ds(0, 384)], recv_kx)
    for d in range(1, Y):
        remote(kern.at[second], kern.at[second], send_k, recv_ky.at[d], y=y_at[d]).start()
    remote(kern.at[second], kern.at[second], send_k, recv_kc.at[0], c=1 - c).start()
    lax.fori_loop(4, Z - AHEAD, step, 0)
    for t in range(Z - AHEAD, Z):
        onward(t)

    loads = [
        pltpu.make_async_copy(wide_hbm, wide, tab_sem.at[0]),
        pltpu.make_async_copy(square_hbm, square, tab_sem.at[1]),
        pltpu.make_async_copy(turn_hbm, turn, tab_sem.at[2]),
    ]
    for table in loads:
        table.start()
    for d in range(1, Y):
        view = kern.at[pl.ds(pl.multiple_of(y_at[Y - d] * 1024 + c * 512, 512), 512)]
        wait_bytes(view, recv_ky.at[d])
        remote(view, view, send_k, recv_kc.at[d], c=1 - c).start()
    for k in range(len(FAR)):
        slot = (Z - FAR[k]) * PLANE + mine
        wait_bytes(far.at[k], recv_far.at[k])
        for p in range(1, PLANE):
            xx, cc = plane_at[p]
            remote(far.at[k, xx * C + cc], rows.at[slot], send_p, recv_out, x=xx, c=cc).start()
        rows[slot] = far[k, mine]
    for table in loads:
        table.wait()
    for d in range(Y):
        wait_bytes(kern.at[pl.ds(0, 512)], recv_kc.at[d])

    first = []
    for part in range(2):
        t = jnp.concatenate(
            [
                jnp.concatenate(
                    [kern[pl.ds(yy * 1024 + part * 4 + jj, 128, stride=8), :] for jj in range(4)], axis=0
                )
                for yy in range(Y)
            ],
            axis=1,
        )
        high, low = split(t)
        dims = (((1,), (1,)), ((), ()))
        pick = square[pl.ds(3072, 2 * U), :]
        picked = lax.dot_general(pick, high, dims, preferred_element_type=F32)
        picked = picked + lax.dot_general(pick, low, dims, preferred_element_type=F32)
        first.append(picked)
    for sign in range(2):
        stack = jnp.concatenate([f[sign * U:(sign + 1) * U] for f in first], axis=0)
        high, low = split(stack)
        place = square[pl.ds(2048 + sign * DET, DET), :]
        moved = mul(high, place) + mul(low, place)
        if sign == 0:
            folded[...] = moved
        else:
            folded[pl.ds(0, U), :] += moved[:U]
            folded[pl.ds(U, U), :] -= moved[U:]

    def over_rows(g):
        high, low = split(rows[pl.ds(g * 64, 64)].reshape(HALF, DET))
        w_high = wide[pl.ds(g * 4 * U, 2 * U), :]
        w_low = wide[pl.ds(g * 4 * U + 2 * U, 2 * U), :]
        return mul(w_high, high) + mul(w_high, low) + mul(w_low, high)

    wait_bytes(rows.at[pl.ds(0, len(FAR) * (PLANE - 1))], recv_out)
    wait_bytes(rows.at[pl.ds(0, 40)], recv_z.at[0])
    spec[...] = over_rows(0)
    wait_bytes(rows.at[pl.ds(0, 48)], recv_z.at[1])
    total = spec[...] + over_rows(1)

    t_high, t_low = square[pl.ds(0, DET), :], square[pl.ds(DET, DET), :]
    tc, ts = turn[0:1, :HALF], turn[0:1, HALF:]

    def two(first, second):
        high, low = split(jnp.concatenate([jnp.concatenate(first, axis=1), jnp.concatenate(second, axis=1)], axis=0))
        full = mul(high, t_high) + mul(low, t_high) + mul(high, t_low)
        return full[:U, :HALF], full[:U, HALF:], full[U:, :HALF], full[U:, HALF:]

    re, im = total[:U], total[U:]
    a_re, a_im = re[:, :HALF] + re[:, HALF:], im[:, :HALF] + im[:, HALF:]
    b_re, b_im = re[:, :HALF] - re[:, HALF:], im[:, :HALF] - im[:, HALF:]
    a_re, a_im, o_re, o_im = two([a_re, a_im], [b_re * tc + b_im * ts, b_im * tc - b_re * ts])
    k_re, k_im = folded[pl.ds(0, U), pl.ds(0, HALF)], folded[pl.ds(U, U), pl.ds(0, HALF)]
    l_re, l_im = folded[pl.ds(0, U), pl.ds(HALF, HALF)], folded[pl.ds(U, U), pl.ds(HALF, HALF)]
    a_im, a_re, o_im, o_re = two(
        [a_re * k_im + a_im * k_re, a_re * k_re - a_im * k_im],
        [o_re * l_im + o_im * l_re, o_re * l_re - o_im * l_im],
    )
    b_re, b_im = o_re * tc - o_im * ts, o_im * tc + o_re * ts
    middle = (a_re[HALF:HALF + 1], b_re[HALF:HALF + 1])
    nyquist = jnp.concatenate([middle[0] + middle[1], middle[0] - middle[1]], axis=1) * (1.0 / (DET * DET))
    a_re, a_im, b_re, b_im = (v[:HALF] for v in (a_re, a_im, b_re, b_im))
    stack = jnp.concatenate(
        [
            jnp.concatenate([a_re + b_re, a_re - b_re], axis=1),
            jnp.concatenate([a_im + b_im, a_im - b_im], axis=1),
        ],
        axis=0,
    )
    high, low = split(stack)
    i_high, i_low = square[pl.ds(1024, DET), :], square[pl.ds(1536, DET), :]
    result = mul(i_high, high) + mul(i_high, low) + mul(i_low, high)
    even, odd = result[:HALF] + nyquist, result[HALF:] - nyquist
    for t in range(4):
        plane[t, pl.ds(0, HALF), :] = even[:, t * 128:(t + 1) * 128]
        plane[t, pl.ds(HALF, HALF), :] = odd[:, t * 128:(t + 1) * 128]

    wait_bytes(staged.at[pl.ds(0, 112)], send_p)
    wait_bytes(mid.at[pl.ds(0, 120)], send_z)
    wait_bytes(kern.at[pl.ds(0, 120)], send_k)
    wait_bytes(kern.at[pl.ds(0, 384)], send_k)
    wait_bytes(kern.at[pl.ds(0, 3584)], send_k)


def select(owner_frame, ids, counts, plane, out, slots):
    z, x, c = (lax.axis_index(a) for a in STRIP)
    own = owner_frame[(z * X + x) * C + c]
    count = counts[own]
    left = lax.broadcasted_iota(jnp.int32, (16, 128), 1) < 64
    for m in range(MAXB):
        b = jnp.where(m < count, ids[m, own], 0)
        rb, cb = lax.div(b, NB), lax.rem(b, NB)
        lane_tile, lane_half = lax.div(cb, 2), lax.rem(cb, 2)
        for part in range(2):
            start = pl.multiple_of(lax.rem(rb * 32 + (Z - z) * 16 + part * 16, HALF), 16)
            e = plane[lane_tile, pl.ds(start, 16), :]
            o = plane[lane_tile, pl.ds(start + HALF, 16), :]
            low_pair = jnp.where(left, e, pltpu.roll(o, 64, 1))
            high_pair = jnp.where(left, pltpu.roll(e, 64, 1), o)
            pair = jnp.where(lane_half == 0, low_pair, high_pair)
            slots[pl.ds(m * 32 + part * 16, 16), :] = jnp.where(m < count, pair, 0.0)
    for r in range(32):
        out[:, pl.ds(r * 128, 128)] = slots[pl.ds(r, MAXB, stride=32), :]


def shards(frames, kernel, owner_rank, block_ids, block_counts):
    rank = owner_rank.reshape(-1)
    place = jnp.arange(STRIPS, dtype=jnp.int32)
    owner_frame = jnp.sum(jnp.where(rank[None, :] == place[:, None], place[None, :], 0), axis=1)
    wide, square, turn = tables()
    hbm = pl.BlockSpec(memory_space=pltpu.HBM)
    smem = pl.BlockSpec(memory_space=pltpu.SMEM)
    vmem = pl.BlockSpec(memory_space=pltpu.VMEM)
    dma = pltpu.SemaphoreType.DMA
    strips = (STRIPS, 4, DET)
    def in_hbm(array):
        return pltpu.with_memory_space_constraint(array, pltpu.HBM)

    plane = pl.pallas_call(
        body,
        name="correlate",
        out_shape=pltpu.VMEM((4, DET, 128), F32),
        in_specs=[smem, hbm, hbm, hbm, hbm, hbm],
        out_specs=vmem,
        scratch_shapes=[
            pltpu.VMEM(strips, F32),
            pltpu.VMEM(strips, F32),
            pltpu.VMEM(strips, F32),
            pltpu.VMEM((len(FAR), PLANE, 4, DET), F32),
            pltpu.VMEM(strips, F32),
            pltpu.VMEM((4096, 128), F32),
            pltpu.VMEM(wide.shape, BF16),
            pltpu.VMEM(square.shape, BF16),
            pltpu.VMEM(turn.shape, F32),
            pltpu.VMEM((2 * U, DET), F32),
            pltpu.VMEM((2 * U, DET), F32),
            dma((2,)), dma((3,)), dma, dma((Z,)), dma, dma((2,)), dma((len(FAR),)), dma, dma, dma, dma, dma((Y,)), dma((Y,)),
        ],
        compiler_params=pltpu.CompilerParams(
            collective_id=0, has_side_effects=True, vmem_limit_bytes=50 << 20
        ),
    )(
        owner_frame,
        in_hbm(frames),
        in_hbm(kernel.transpose(0, 2, 1).reshape(8, 128)),
        in_hbm(jnp.asarray(wide)),
        in_hbm(jnp.asarray(square)),
        in_hbm(jnp.asarray(turn)),
    )
    result = pl.pallas_call(
        select,
        name="select",
        out_shape=jax.ShapeDtypeStruct((MAXB, 4096), F32),
        in_specs=[smem, smem, smem, vmem],
        out_specs=vmem,
        scratch_shapes=[pltpu.VMEM((MAXB * 32, 128), F32)],
        compiler_params=pltpu.CompilerParams(vmem_limit_bytes=4 << 20),
    )(owner_frame, block_ids.T, block_counts, plane)
    return result[None]


def solution(mesh):
    finer = Mesh(mesh.devices.reshape(Z, X, C, Y), ("z", "x", "c", "y"))
    in_specs = (
        P("y", STRIP, None),
        P(None, "y", STRIP),
        P("y", None),
        P("y", None),
        P("y"),
    )
    return jax.shard_map(
        shards, mesh=finer, in_specs=in_specs, out_specs=P(STRIP, "y", None), check_vma=False
    )
```

```python
import functools

import jax
import jax.numpy as jnp
import ml_dtypes
import numpy as np
from jax import lax
from jax.experimental import pallas as pl
from jax.experimental.pallas import tpu as pltpu
from jax.sharding import Mesh
from jax.sharding import PartitionSpec as P

DET = 512
HALF = DET // 2
NB = 8
MAXB = 16
Z, X, C, Y = 16, 4, 2, 4
PLANE = X * C
STRIPS = Z * PLANE
STRIP = ("z", "x", "c")
U = 272
AHEAD = 9
FAR = (8, 9, 7)
F32 = jnp.float32
BF16 = jnp.bfloat16
MESH = pl.DeviceIdType.MESH


def halves(table):
    high = table.astype(ml_dtypes.bfloat16)
    low = (table - high.astype(np.float64)).astype(ml_dtypes.bfloat16)
    return high, low


def tables():
    n = np.arange(DET)
    angle = 2.0 * np.pi / DET
    u = np.arange(U)
    used = (u <= HALF).astype(np.float64)[:, None]
    phase = (u[:, None] * n[None, :]) % DET * angle
    forward = np.concatenate([np.cos(phase) * used, -np.sin(phase) * used])
    forward = forward.reshape(2 * U, 2, HALF).transpose(1, 0, 2)
    j = np.arange(HALF)
    small = (j[:, None] * j[None, :]) % HALF * (2.0 * angle)
    square = np.block([[np.cos(small), -np.sin(small)], [np.sin(small), np.cos(small)]])
    turn = np.zeros((8, DET))
    turn[0] = np.concatenate([np.cos(j * angle), np.sin(j * angle)])
    out_rows = np.concatenate([n[0::2], n[1::2]])
    weight = np.where(j == 0, 1.0, 2.0) / (DET * DET)
    back = (out_rows[:, None] * j[None, :]) % DET * angle
    inverse = np.concatenate([np.cos(back) * weight, -np.sin(back) * weight], axis=1)
    jj, cc, xx, zz = np.meshgrid(np.arange(4), np.arange(C), np.arange(X), np.arange(Z), indexing="ij")
    v_in = (4 * (8 * zz + 2 * xx + cc) + jj).reshape(-1)
    v_out = np.concatenate([n[0::2], n[1::2]])
    pick = np.concatenate(
        [(n[None, :] == u[:, None]) * used, (n[None, :] == (-u[:, None]) % DET) * used]
    )
    place = np.concatenate(
        [v_in[:, None] == v_out[None, :], v_in[:, None] == (-v_out[None, :]) % DET]
    )
    wide = np.concatenate([*halves(forward[0]), *halves(forward[1])])
    return (
        wide,
        np.concatenate([*halves(square), *halves(inverse), (0.5 * place).astype(ml_dtypes.bfloat16),
                        pick.astype(ml_dtypes.bfloat16)]),
        turn.astype(np.float32),
    )


def remote(src, dst, send_sem, recv_sem, **where):
    return pltpu.make_async_remote_copy(
        src_ref=src, dst_ref=dst, send_sem=send_sem, recv_sem=recv_sem, device_id=where, device_id_type=MESH
    )


def wait_bytes(view, sem):
    pltpu.make_async_copy(view, view, sem).wait()


def split(value):
    high = value.astype(BF16)
    return high, (value - high.astype(F32)).astype(BF16)


def mul(left, right):
    return jnp.dot(left, right, preferred_element_type=F32)


def body(owner_frame, frames_hbm, kernel_hbm, wide_hbm, square_hbm, turn_hbm, plane,
         frames, staged, mid, far, rows, kern, wide, square, turn, spec, folded,
         in_sem, tab_sem, send_p, recv_p, send_z, recv_z, recv_far, recv_out, send_k, recv_kz, recv_kx, recv_ky, recv_kc):
    z, x, c, y = (lax.axis_index(a) for a in ("z", "x", "c", "y"))
    mine = x * C + c
    z_at = [z] + [lax.rem(z + d, Z) for d in range(1, Z)]
    y_at = [y] + [lax.rem(y + d, Y) for d in range(1, Y)]
    x_at = [x] + [lax.rem(x + d, X) for d in range(1, X)]
    plane_at = [(x_at[p // C], (c, 1 - c)[p % C]) for p in range(PLANE)]
    load = pltpu.make_async_copy(frames_hbm, frames, in_sem.at[0])
    load.start()
    own_rows = pl.ds(pl.multiple_of(y * 1024 + ((c * X + x) * Z + z) * 8, 8), 8)
    load_kernel = pltpu.make_async_copy(kernel_hbm, kern.at[own_rows], in_sem.at[1])
    load_kernel.start()

    peers = [{"z": z_at[d]} for d in range(1, Z)]
    peers += [{"x": xx, "c": cc} for xx, cc in plane_at[1:]]
    peers += [{"y": y_at[d]} for d in range(1, Y)]
    barrier = pltpu.get_barrier_semaphore()
    for peer in peers:
        pl.semaphore_signal(barrier, inc=1, device_id=peer, device_id_type=MESH)
    pl.semaphore_wait(barrier, len(peers))

    load_kernel.wait()
    for d in range(1, Z):
        remote(kern.at[own_rows], kern.at[own_rows], send_k, recv_kz, z=z_at[d]).start()
    load.wait()

    def far_first(k):
        there = z_at[FAR[k]]
        for p in range(PLANE):
            staged[there * PLANE + p] = frames[owner_frame[there * PLANE + p]]
        remote(staged.at[pl.ds(there * PLANE, PLANE)], far.at[k], send_z, recv_far.at[k], z=there).start()

    def is_near(t):
        away = (t - z + Z) % Z
        near = away != FAR[0]
        for d in FAR[1:]:
            near = jnp.logical_and(near, away != d)
        return near

    def target_of(k):
        i = k % 8
        return (z + Z + (i + 1) // 2 * (1 - 2 * (i % 2))) % (Z // 2) + Z // 2 * (k // (Z // 2))

    def to_plane(k):
        t = target_of(k)

        @pl.when(is_near(t))
        def _():
            for p in range(1, PLANE):
                xx, cc = plane_at[p]
                slot = t * PLANE + xx * C + cc
                staged[slot] = frames[owner_frame[slot]]
                remote(staged.at[slot], mid.at[t * PLANE + mine], send_p, recv_p.at[t], x=xx, c=cc).start()
            mid[t * PLANE + mine] = frames[owner_frame[t * PLANE + mine]]

    def onward(k):
        t = target_of(k)

        @pl.when(is_near(t))
        def _():
            piece = pl.ds(t * PLANE, PLANE)
            wait_bytes(mid.at[pl.ds(t * PLANE, PLANE - 1)], recv_p.at[t])
            slot = (z - t + Z) % Z

            @pl.when(t != z)
            def _():
                target = rows.at[pl.ds(slot * PLANE, PLANE)]
                remote(mid.at[piece], target, send_z, recv_z.at[slot // 8], z=t).start()

            @pl.when(t == z)
            def _():
                rows[pl.ds(0, PLANE)] = mid[piece]

    def step(t, carry):
        to_plane(t + AHEAD)
        onward(t)
        return carry

    for k in range(len(FAR)):
        far_first(k)
    for t in range(AHEAD):
        to_plane(t)
    lax.fori_loop(0, 2, step, 0)
    third = pl.ds(pl.multiple_of(y * 1024 + (c * X + x) * 128, 128), 128)
    wait_bytes(kern.at[pl.ds(0, 120)], recv_kz)
    for d in range(1, X):
        remote(kern.at[third], kern.at[third], send_k, recv_kx, x=x_at[d]).start()
    lax.fori_loop(2, 4, step, 0)
    second = pl.ds(pl.multiple_of(y * 1024 + c * 512, 512), 512)
    wait_bytes(kern.at[pl.ds(0, 384)], recv_kx)
    for d in range(1, Y):
        remote(kern.at[second], kern.at[second], send_k, recv_ky.at[d], y=y_at[d]).start()
    remote(kern.at[second], kern.at[second], send_k, recv_kc.at[0], c=1 - c).start()
    lax.fori_loop(4, Z - AHEAD, step, 0)
    for t in range(Z - AHEAD, Z):
        onward(t)

    loads = [
        pltpu.make_async_copy(wide_hbm, wide, tab_sem.at[0]),
        pltpu.make_async_copy(square_hbm, square, tab_sem.at[1]),
        pltpu.make_async_copy(turn_hbm, turn, tab_sem.at[2]),
    ]
    for table in loads:
        table.start()
    for d in range(1, Y):
        view = kern.at[pl.ds(pl.multiple_of(y_at[Y - d] * 1024 + c * 512, 512), 512)]
        wait_bytes(view, recv_ky.at[d])
        remote(view, view, send_k, recv_kc.at[d], c=1 - c).start()
    for k in range(len(FAR)):
        slot = (Z - FAR[k]) * PLANE + mine
        wait_bytes(far.at[k], recv_far.at[k])
        for p in range(1, PLANE):
            xx, cc = plane_at[p]
            remote(far.at[k, xx * C + cc], rows.at[slot], send_p, recv_out, x=xx, c=cc).start()
        rows[slot] = far[k, mine]
    for table in loads:
        table.wait()
    for d in range(Y):
        wait_bytes(kern.at[pl.ds(0, 512)], recv_kc.at[d])

    first = []
    for part in range(2):
        t = jnp.concatenate(
            [
                jnp.concatenate(
                    [kern[pl.ds(yy * 1024 + part * 4 + jj, 128, stride=8), :] for jj in range(4)], axis=0
                )
                for yy in range(Y)
            ],
            axis=1,
        )
        high, low = split(t)
        dims = (((1,), (1,)), ((), ()))
        pick = square[pl.ds(3072, 2 * U), :]
        picked = lax.dot_general(pick, high, dims, preferred_element_type=F32)
        picked = picked + lax.dot_general(pick, low, dims, preferred_element_type=F32)
        first.append(picked)
    for sign in range(2):
        stack = jnp.concatenate([f[sign * U:(sign + 1) * U] for f in first], axis=0)
        high, low = split(stack)
        place = square[pl.ds(2048 + sign * DET, DET), :]
        moved = mul(high, place) + mul(low, place)
        if sign == 0:
            folded[...] = moved
        else:
            folded[pl.ds(0, U), :] += moved[:U]
            folded[pl.ds(U, U), :] -= moved[U:]

    def over_rows(g):
        high, low = split(rows[pl.ds(g * 64, 64)].reshape(HALF, DET))
        w_high = wide[pl.ds(g * 4 * U, 2 * U), :]
        w_low = wide[pl.ds(g * 4 * U + 2 * U, 2 * U), :]
        return mul(w_high, high) + mul(w_high, low) + mul(w_low, high)

    wait_bytes(rows.at[pl.ds(0, len(FAR) * (PLANE - 1))], recv_out)
    wait_bytes(rows.at[pl.ds(0, 48)], recv_z.at[0])
    spec[...] = over_rows(0)
    wait_bytes(rows.at[pl.ds(0, 48)], recv_z.at[1])
    total = spec[...] + over_rows(1)

    t_high, t_low = square[pl.ds(0, DET), :], square[pl.ds(DET, DET), :]
    tc, ts = turn[0:1, :HALF], turn[0:1, HALF:]

    def two(first, second):
        high, low = split(jnp.concatenate([jnp.concatenate(first, axis=1), jnp.concatenate(second, axis=1)], axis=0))
        full = mul(high, t_high) + mul(low, t_high) + mul(high, t_low)
        return full[:U, :HALF], full[:U, HALF:], full[U:, :HALF], full[U:, HALF:]

    re, im = total[:U], total[U:]
    a_re, a_im = re[:, :HALF] + re[:, HALF:], im[:, :HALF] + im[:, HALF:]
    b_re, b_im = re[:, :HALF] - re[:, HALF:], im[:, :HALF] - im[:, HALF:]
    a_re, a_im, o_re, o_im = two([a_re, a_im], [b_re * tc + b_im * ts, b_im * tc - b_re * ts])
    k_re, k_im = folded[pl.ds(0, U), pl.ds(0, HALF)], folded[pl.ds(U, U), pl.ds(0, HALF)]
    l_re, l_im = folded[pl.ds(0, U), pl.ds(HALF, HALF)], folded[pl.ds(U, U), pl.ds(HALF, HALF)]
    a_im, a_re, o_im, o_re = two(
        [a_re * k_im + a_im * k_re, a_re * k_re - a_im * k_im],
        [o_re * l_im + o_im * l_re, o_re * l_re - o_im * l_im],
    )
    b_re, b_im = o_re * tc - o_im * ts, o_im * tc + o_re * ts
    middle = (a_re[HALF:HALF + 1], b_re[HALF:HALF + 1])
    nyquist = jnp.concatenate([middle[0] + middle[1], middle[0] - middle[1]], axis=1) * (1.0 / (DET * DET))
    a_re, a_im, b_re, b_im = (v[:HALF] for v in (a_re, a_im, b_re, b_im))
    stack = jnp.concatenate(
        [
            jnp.concatenate([a_re + b_re, a_re - b_re], axis=1),
            jnp.concatenate([a_im + b_im, a_im - b_im], axis=1),
        ],
        axis=0,
    )
    high, low = split(stack)
    i_high, i_low = square[pl.ds(1024, DET), :], square[pl.ds(1536, DET), :]
    result = mul(i_high, high) + mul(i_high, low) + mul(i_low, high)
    even, odd = result[:HALF] + nyquist, result[HALF:] - nyquist
    for t in range(4):
        plane[t, pl.ds(0, HALF), :] = even[:, t * 128:(t + 1) * 128]
        plane[t, pl.ds(HALF, HALF), :] = odd[:, t * 128:(t + 1) * 128]

    wait_bytes(staged.at[pl.ds(0, 112)], send_p)
    wait_bytes(mid.at[pl.ds(0, 120)], send_z)
    wait_bytes(kern.at[pl.ds(0, 120)], send_k)
    wait_bytes(kern.at[pl.ds(0, 384)], send_k)
    wait_bytes(kern.at[pl.ds(0, 3584)], send_k)


def select(owner_frame, ids, counts, plane, out, slots):
    z, x, c = (lax.axis_index(a) for a in STRIP)
    own = owner_frame[(z * X + x) * C + c]
    count = counts[own]
    left = lax.broadcasted_iota(jnp.int32, (16, 128), 1) < 64
    for m in range(MAXB):
        b = jnp.where(m < count, ids[m, own], 0)
        rb, cb = lax.div(b, NB), lax.rem(b, NB)
        lane_tile, lane_half = lax.div(cb, 2), lax.rem(cb, 2)
        for part in range(2):
            start = pl.multiple_of(lax.rem(rb * 32 + (Z - z) * 16 + part * 16, HALF), 16)
            e = plane[lane_tile, pl.ds(start, 16), :]
            o = plane[lane_tile, pl.ds(start + HALF, 16), :]
            low_pair = jnp.where(left, e, pltpu.roll(o, 64, 1))
            high_pair = jnp.where(left, pltpu.roll(e, 64, 1), o)
            pair = jnp.where(lane_half == 0, low_pair, high_pair)
            slots[pl.ds(m * 32 + part * 16, 16), :] = jnp.where(m < count, pair, 0.0)
    for r in range(32):
        out[:, pl.ds(r * 128, 128)] = slots[pl.ds(r, MAXB, stride=32), :]


def shards(frames, kernel, owner_rank, block_ids, block_counts):
    rank = owner_rank.reshape(-1)
    place = jnp.arange(STRIPS, dtype=jnp.int32)
    owner_frame = jnp.sum(jnp.where(rank[None, :] == place[:, None], place[None, :], 0), axis=1)
    wide, square, turn = tables()
    hbm = pl.BlockSpec(memory_space=pltpu.HBM)
    smem = pl.BlockSpec(memory_space=pltpu.SMEM)
    vmem = pl.BlockSpec(memory_space=pltpu.VMEM)
    dma = pltpu.SemaphoreType.DMA
    strips = (STRIPS, 4, DET)
    def in_hbm(array):
        return pltpu.with_memory_space_constraint(array, pltpu.HBM)

    plane = pl.pallas_call(
        body,
        name="correlate",
        out_shape=pltpu.VMEM((4, DET, 128), F32),
        in_specs=[smem, hbm, hbm, hbm, hbm, hbm],
        out_specs=vmem,
        scratch_shapes=[
            pltpu.VMEM(strips, F32),
            pltpu.VMEM(strips, F32),
            pltpu.VMEM(strips, F32),
            pltpu.VMEM((len(FAR), PLANE, 4, DET), F32),
            pltpu.VMEM(strips, F32),
            pltpu.VMEM((4096, 128), F32),
            pltpu.VMEM(wide.shape, BF16),
            pltpu.VMEM(square.shape, BF16),
            pltpu.VMEM(turn.shape, F32),
            pltpu.VMEM((2 * U, DET), F32),
            pltpu.VMEM((2 * U, DET), F32),
            dma((2,)), dma((3,)), dma, dma((Z,)), dma, dma((2,)), dma((len(FAR),)), dma, dma, dma, dma, dma((Y,)), dma((Y,)),
        ],
        compiler_params=pltpu.CompilerParams(
            collective_id=0, has_side_effects=True, vmem_limit_bytes=50 << 20
        ),
    )(
        owner_frame,
        in_hbm(frames),
        in_hbm(kernel.transpose(0, 2, 1).reshape(8, 128)),
        in_hbm(jnp.asarray(wide)),
        in_hbm(jnp.asarray(square)),
        in_hbm(jnp.asarray(turn)),
    )
    result = pl.pallas_call(
        select,
        name="select",
        out_shape=jax.ShapeDtypeStruct((MAXB, 4096), F32),
        in_specs=[smem, smem, smem, vmem],
        out_specs=vmem,
        scratch_shapes=[pltpu.VMEM((MAXB * 32, 128), F32)],
        compiler_params=pltpu.CompilerParams(vmem_limit_bytes=4 << 20),
    )(owner_frame, block_ids.T, block_counts, plane)
    return result[None]


def solution(mesh):
    finer = Mesh(mesh.devices.reshape(Z, X, C, Y), ("z", "x", "c", "y"))
    in_specs = (
        P("y", STRIP, None),
        P(None, "y", STRIP),
        P("y", None),
        P("y", None),
        P("y"),
    )
    return jax.shard_map(
        shards, mesh=finer, in_specs=in_specs, out_specs=P(STRIP, "y", None), check_vma=False
    )
```
